512 devices in a mesh: tok: 16 (over z, core), voc: 32 (over y, x).
Axes of the slice: x: 4, y: 8, z: 8, core: 2. Of those that a mesh axis runs over, the one named last changes fastest.
Arguments:
- hidden: bfloat16 [256, 2304], P('tok', 'voc'), may hold values from -18 to 18
- head: bfloat16 [2304, 131072], P(None, ('tok', 'voc')), as said below
- targets: int32 [256], replicated, may hold values from 0 to 131071
- probe_hidden: bfloat16 [256, 2304], P('tok', 'voc'), may hold values from -6 to 6
- probe_head: bfloat16 [2304, 131072], P(None, ('tok', 'voc')), may hold values from -0.5 to 0.5
Outputs:
- head_out: float32 [2304, 131072], P(None, ('tok', 'voc'))
- hidden_out: float32 [256, 2304], P('tok', 'voc')
The draws below stay inside these ranges and needn't reach their ends.
Inputs may be any that keep to these rules, and one draw needn't show every extreme that they name: `head`: entries lie within 66 / sqrt(2304) in magnitude.
All inputs are finite; a program needn't handle non-finite values.
Results may differ from the reference program's by a relative error of at most 0.0075.
Values may be sent and summed in bfloat16 or wider, within the bound.
A program may use at most 64 MiB of HBM per device.

```python
import jax
import jax.numpy as jnp

D = 2304
TOKENS = 256
VOCAB = 131072


def draw_hidden(key, part):
    key_scale = jax.random.fold_in(jax.random.fold_in(key, 11), 0)
    key_noise = jax.random.fold_in(jax.random.fold_in(key, 11), 2)
    row_scale = jnp.exp(jax.random.uniform(key_scale, (TOKENS, 1), jnp.float32, -1.15, 1.15))
    values = row_scale * jax.random.truncated_normal(key_noise, -4.0, 4.0, (TOKENS, D), jnp.float32)
    return values.astype(jnp.bfloat16)


def draw_head(key, part):
    key_scale = jax.random.fold_in(jax.random.fold_in(key, 23), 0)
    key_noise = jax.random.fold_in(jax.random.fold_in(key, 23), 2)
    ramp = 0.75 + 0.5 * jnp.arange(VOCAB, dtype=jnp.float32)[None, :] / VOCAB
    base = 3.0 / jnp.sqrt(jnp.float32(D))
    col_scale = jnp.exp(jax.random.uniform(key_scale, (1, VOCAB), jnp.float32, -1.15, 1.15)) * ramp
    values = base * col_scale * jax.random.truncated_normal(key_noise, -4.0, 4.0, (D, VOCAB), jnp.float32)
    return values.astype(jnp.bfloat16)


def plant(drawn, own_key, least, top_value):
    longest = drawn.shape.index(max(drawn.shape))
    spots = []
    for shift in (0, 1):
        where = [jax.random.randint(jax.random.fold_in(own_key, axis), (), 0, length) for axis, length in enumerate(drawn.shape)]
        where[longest] = (where[longest] + shift) % drawn.shape[longest]
        spots.append(tuple(where))
    return drawn.at[spots[0]].set(least).at[spots[1]].set(top_value)


def spiked(drawn, own_key, source, target, blocks, factor):
    def block_of(axis_at):
        return (jnp.arange(drawn.shape[axis_at]) // (drawn.shape[axis_at] // blocks)).reshape((-1,) + (1,) * (drawn.ndim - 1 - axis_at))

    near = jax.random.permutation(own_key, blocks)[block_of(target)]
    other_side = (block_of(target) + blocks // 2) % blocks
    return jnp.where((block_of(source) == near) | (block_of(source) == other_side), factor * drawn, drawn)


def levels(stream_key, dims, cuts, least, high):
    def one(dim, blocks):
        steps = jax.random.uniform(jax.random.fold_in(jax.random.fold_in(stream_key, 6), dim), (blocks,), jnp.float32, least / len(cuts), high / len(cuts))
        return jnp.repeat(jnp.exp(steps), dims[dim] // blocks).reshape((-1,) + (1,) * (len(dims) - dim - 1))

    loudness = one(*cuts[0])
    for cut in cuts[1:]:
        loudness = loudness * one(*cut)
    return loudness


def normal_values(rng, shape, spread, bound, cuts=(), held_as=jnp.bfloat16):
    drawn = spread * jax.random.normal(rng, shape, jnp.float32)
    if cuts:
        drawn = drawn * levels(rng, shape, cuts, -0.22, 0.18)
    return jnp.clip(drawn, -bound, bound).astype(held_as)


def heavy_noise(key, extent, width, reach, pieces, heavy, kind=jnp.bfloat16):
    array = width * jax.random.normal(key, extent, jnp.float32)
    if pieces:
        array = array * levels(key, extent, pieces, -0.22, 0.18)
    return jnp.clip(spiked(array, jax.random.fold_in(key, 3), *heavy), -reach, reach).astype(kind)


def setup_inputs(seed: int = 0) -> dict:
    key_of = jax.random.split(jax.random.key(seed), 6)
    hidden = draw_hidden(jax.random.fold_in(key_of[5], 71), 0)
    head = draw_head(jax.random.fold_in(key_of[5], 71), 0)
    targets = plant(jax.random.randint(key_of[2], (TOKENS,), 0, VOCAB), jax.random.fold_in(key_of[2], 1), 0, VOCAB - 1).astype(jnp.int32)
    probe_hidden = normal_values(key_of[3], (TOKENS, D), 1.0, 6.0, ((0, 16), (1, 32)))
    probe_head = heavy_noise(key_of[4], (D, VOCAB), D ** -0.5, 0.5, ((1, 512),), (1, 0, 256, 6.0))
    return {"hidden": hidden, "head": head, "targets": targets, "probe_hidden": probe_hidden, "probe_head": probe_head}


softcap_value = 30.0
zloss_weight = 1e-4


def reference(hidden, head, targets, probe_hidden, probe_head):
    logits = jnp.dot(hidden, head, preferred_element_type=jnp.float32)
    tangent = jnp.dot(probe_hidden, head, preferred_element_type=jnp.float32) + jnp.dot(hidden, probe_head, preferred_element_type=jnp.float32)
    capped = jnp.tanh(logits / softcap_value)
    cap_slope = 1.0 - capped * capped
    exponent = jnp.exp(softcap_value * capped)
    row_total = jnp.sum(exponent, axis=1)
    probability = exponent / row_total[:, None]
    cap_tangent = cap_slope * tangent
    mean_tangent = jnp.sum(probability * cap_tangent, axis=1)
    factor = 1.0 + 2.0 * zloss_weight * jnp.log(row_total)
    columns = jnp.arange(VOCAB, dtype=jnp.int32)
    onehot = (targets[:, None] == columns[None, :]).astype(jnp.float32)
    grad_cap = factor[:, None] * probability - onehot
    grad_tan = probability * (factor[:, None] * (cap_tangent - mean_tangent[:, None]) + 2.0 * zloss_weight * mean_tangent[:, None])
    slope_tan = (-2.0 / softcap_value) * capped * cap_slope * tangent
    dlogit = (grad_cap * cap_slope).astype(jnp.bfloat16)
    dlogit_tan = (grad_tan * cap_slope + grad_cap * slope_tan).astype(jnp.bfloat16)
    head_out = jnp.dot(probe_hidden.T, dlogit, preferred_element_type=jnp.float32) + jnp.dot(hidden.T, dlogit_tan, preferred_element_type=jnp.float32)
    hidden_out = jnp.dot(dlogit, probe_head.T, preferred_element_type=jnp.float32) + jnp.dot(dlogit_tan, head.T, preferred_element_type=jnp.float32)
    return head_out, hidden_out
```

```python
import jax
import jax.numpy as jnp
from jax import lax
from jax.sharding import PartitionSpec as P

softcap_value = 30.0
zloss_weight = 0.0001


def local(hidden, head, targets, probe_hidden, probe_head):
    voc_count = lax.axis_size("voc")
    vocab_width = head.shape[1]
    stacked = jnp.stack([hidden, probe_hidden])
    features = lax.all_gather(stacked, "voc", axis=2, tiled=True)
    gathered = lax.all_gather(features, "tok", axis=1, tiled=True)
    row_hidden = gathered[0]
    row_probe = gathered[1]
    logits = jnp.dot(row_hidden, head, preferred_element_type=jnp.float32)
    tangent = jnp.dot(row_probe, head, preferred_element_type=jnp.float32) + jnp.dot(
        row_hidden, probe_head, preferred_element_type=jnp.float32
    )
    capped = jnp.tanh(logits / softcap_value)
    cap_slope = 1.0 - capped * capped
    exponent = jnp.exp(softcap_value * capped)
    cap_tangent = cap_slope * tangent
    stats = lax.psum(
        jnp.stack([jnp.sum(exponent, axis=1), jnp.sum(exponent * cap_tangent, axis=1)]),
        ("tok", "voc"),
    )
    row_total = stats[0]
    probability = exponent / row_total[:, None]
    mean_tangent = stats[1] / row_total
    factor = 1.0 + 2.0 * zloss_weight * jnp.log(row_total)
    offset = (lax.axis_index("tok") * voc_count + lax.axis_index("voc")) * vocab_width
    columns = offset + lax.iota(jnp.int32, vocab_width)
    onehot = (targets[:, None] == columns[None, :]).astype(jnp.float32)
    grad_cap = factor[:, None] * probability - onehot
    grad_tan = probability * (
        factor[:, None] * (cap_tangent - mean_tangent[:, None])
        + 2.0 * zloss_weight * mean_tangent[:, None]
    )
    slope_tan = -2.0 / softcap_value * capped * cap_slope * tangent
    dlogit = (grad_cap * cap_slope).astype(jnp.bfloat16)
    dlogit_tan = (grad_tan * cap_slope + grad_cap * slope_tan).astype(jnp.bfloat16)
    head_out = jnp.einsum(
        "krd,krv->dv", gathered, jnp.stack([dlogit_tan, dlogit]), preferred_element_type=jnp.float32
    )
    probe_part = lax.dot_general(
        dlogit, probe_head, (((1,), (1,)), ((), ())), preferred_element_type=jnp.float32
    )
    head_part = lax.dot_general(
        dlogit_tan, head, (((1,), (1,)), ((), ())), preferred_element_type=jnp.float32
    )
    summed = lax.psum_scatter(probe_part + head_part, "tok", scatter_dimension=0, tiled=True)
    hidden_out = lax.psum_scatter(summed, "voc", scatter_dimension=1, tiled=True)
    return (head_out, hidden_out)


def solution(mesh):
    return jax.shard_map(
        local,
        mesh=mesh,
        in_specs=(
            P("tok", "voc"),
            P(None, ("tok", "voc")),
            P(),
            P("tok", "voc"),
            P(None, ("tok", "voc")),
        ),
        out_specs=(P(None, ("tok", "voc")), P("tok", "voc")),
        check_vma=False,
    )
```

```python
import jax
import jax.numpy as jnp
from jax import lax
from jax.sharding import PartitionSpec as P

softcap_value = 30.0
zloss_weight = 0.0001


def local(hidden, head, targets, probe_hidden, probe_head):
    voc_count = lax.axis_size("voc")
    vocab_width = head.shape[1]
    rows_here = hidden.shape[0]
    stacked = jnp.stack([hidden, probe_hidden])
    features = lax.all_gather(stacked, "voc", axis=2, tiled=True)
    gathered = lax.all_gather(features, "tok", axis=1, tiled=True)
    row_hidden = gathered[0]
    row_probe = gathered[1]
    logits = jnp.dot(row_hidden, head, preferred_element_type=jnp.float32)
    tangent = jnp.dot(row_probe, head, preferred_element_type=jnp.float32) + jnp.dot(
        row_hidden, probe_head, preferred_element_type=jnp.float32
    )
    capped = jnp.tanh(logits / softcap_value)
    cap_slope = 1.0 - capped * capped
    exponent = jnp.exp(softcap_value * capped)
    cap_tangent = cap_slope * tangent
    slope_tan = -2.0 / softcap_value * capped * cap_slope * tangent
    offset = (lax.axis_index("tok") * voc_count + lax.axis_index("voc")) * vocab_width
    columns = offset + lax.iota(jnp.int32, vocab_width)
    onehot = (targets[:, None] == columns[None, :]).astype(jnp.float32)

    weighted_slope = exponent * cap_slope
    weighted_tan = exponent * (cap_slope * cap_tangent + slope_tan)
    hi = lax.Precision.HIGHEST
    by_probe = lax.dot_general(
        jnp.stack([weighted_slope, onehot * cap_slope]), probe_head.astype(jnp.float32),
        (((2,), (1,)), ((), ())), precision=hi, preferred_element_type=jnp.float32,
    )
    by_head = lax.dot_general(
        jnp.stack([weighted_tan, weighted_slope, onehot * slope_tan]), head.astype(jnp.float32),
        (((2,), (1,)), ((), ())), precision=hi, preferred_element_type=jnp.float32,
    )
    partials = jnp.stack([by_probe[0] + by_head[0], by_head[1], by_probe[1] + by_head[2]])

    local_stats = jnp.stack([jnp.sum(exponent, axis=1), jnp.sum(exponent * cap_tangent, axis=1)])
    partials, local_stats = lax.optimization_barrier((partials, local_stats))
    summed = lax.psum_scatter(partials, "tok", scatter_dimension=1, tiled=True)
    reduced = lax.psum_scatter(summed, "voc", scatter_dimension=2, tiled=True)
    stats = lax.psum(local_stats, ("tok", "voc"))
    row_total = stats[0]
    probability = exponent / row_total[:, None]
    mean_tangent = stats[1] / row_total
    factor = 1.0 + 2.0 * zloss_weight * jnp.log(row_total)
    grad_cap = factor[:, None] * probability - onehot
    grad_tan = probability * (
        factor[:, None] * (cap_tangent - mean_tangent[:, None])
        + 2.0 * zloss_weight * mean_tangent[:, None]
    )
    dlogit = (grad_cap * cap_slope).astype(jnp.bfloat16)
    dlogit_tan = (grad_tan * cap_slope + grad_cap * slope_tan).astype(jnp.bfloat16)
    head_out = jnp.einsum(
        "krd,krv->dv", gathered, jnp.stack([dlogit_tan, dlogit]), preferred_element_type=jnp.float32
    )

    first_row = lax.axis_index("tok") * rows_here
    own_total = lax.dynamic_slice_in_dim(row_total, first_row, rows_here)
    own_mean = lax.dynamic_slice_in_dim(mean_tangent, first_row, rows_here)
    own_factor = lax.dynamic_slice_in_dim(factor, first_row, rows_here)
    scale_main = (own_factor / own_total)[:, None]
    scale_mean = ((2.0 * zloss_weight - own_factor) * own_mean / own_total)[:, None]
    hidden_out = scale_main * reduced[0] + scale_mean * reduced[1] - reduced[2]
    return (head_out, hidden_out)


def solution(mesh):
    return jax.shard_map(
        local,
        mesh=mesh,
        in_specs=(
            P("tok", "voc"),
            P(None, ("tok", "voc")),
            P(),
            P("tok", "voc"),
            P(None, ("tok", "voc")),
        ),
        out_specs=(P(None, ("tok", "voc")), P("tok", "voc")),
        check_vma=False,
    )
```

```python
import jax
import jax.numpy as jnp
from jax import lax
import numpy as np
from jax.sharding import Mesh, PartitionSpec as P

softcap_value = 30.0
zloss_weight = 0.0001


def local(hidden, head, targets, probe_hidden, probe_head):
    voc_count = lax.axis_size("vy") * lax.axis_size("vx")
    vocab_width = head.shape[1]
    rows_here = hidden.shape[0]
    stacked = jnp.stack([hidden, probe_hidden])
    features = lax.all_gather(lax.all_gather(stacked, "vx", axis=2, tiled=True), "vy", axis=2, tiled=True)
    gathered = lax.all_gather(features, "tok", axis=1, tiled=True)
    row_hidden = gathered[0]
    row_probe = gathered[1]
    logits = jnp.dot(row_hidden, head, preferred_element_type=jnp.float32)
    tangent = jnp.dot(row_probe, head, preferred_element_type=jnp.float32) + jnp.dot(
        row_hidden, probe_head, preferred_element_type=jnp.float32
    )
    capped = jnp.tanh(logits / softcap_value)
    cap_slope = 1.0 - capped * capped
    exponent = jnp.exp(softcap_value * capped)
    cap_tangent = cap_slope * tangent
    slope_tan = -2.0 / softcap_value * capped * cap_slope * tangent
    voc_index = lax.axis_index("vy") * lax.axis_size("vx") + lax.axis_index("vx")
    offset = (lax.axis_index("tok") * voc_count + voc_index) * vocab_width
    columns = offset + lax.iota(jnp.int32, vocab_width)
    onehot = (targets[:, None] == columns[None, :]).astype(jnp.float32)

    weighted_slope = exponent * cap_slope
    weighted_tan = exponent * (cap_slope * cap_tangent + slope_tan)
    hi = lax.Precision.HIGHEST
    by_probe = lax.dot_general(
        jnp.stack([weighted_slope, onehot * cap_slope]), probe_head.astype(jnp.float32),
        (((2,), (1,)), ((), ())), precision=hi, preferred_element_type=jnp.float32,
    )
    by_head = lax.dot_general(
        jnp.stack([weighted_tan, weighted_slope, onehot * slope_tan]), head.astype(jnp.float32),
        (((2,), (1,)), ((), ())), precision=hi, preferred_element_type=jnp.float32,
    )
    partials = jnp.stack([by_probe[0] + by_head[0], by_head[1], by_probe[1] + by_head[2]])

    local_stats = jnp.stack([jnp.sum(exponent, axis=1), jnp.sum(exponent * cap_tangent, axis=1)])
    partials, local_stats = lax.optimization_barrier((partials, local_stats))
    summed = lax.psum_scatter(partials, "tok", scatter_dimension=1, tiled=True)
    stats = lax.psum(lax.psum(lax.psum(local_stats, "tok"), "vy"), "vx")
    kinds, rows, width = summed.shape
    blocks = summed.reshape(kinds, rows, voc_count, width // voc_count).transpose(2, 0, 1, 3)
    reduced = jnp.sum(lax.all_to_all(blocks, ("vy", "vx"), 0, 0, tiled=True), axis=0)
    row_total = stats[0]
    probability = exponent / row_total[:, None]
    mean_tangent = stats[1] / row_total
    factor = 1.0 + 2.0 * zloss_weight * jnp.log(row_total)
    grad_cap = factor[:, None] * probability - onehot
    grad_tan = probability * (
        factor[:, None] * (cap_tangent - mean_tangent[:, None])
        + 2.0 * zloss_weight * mean_tangent[:, None]
    )
    dlogit = (grad_cap * cap_slope).astype(jnp.bfloat16)
    dlogit_tan = (grad_tan * cap_slope + grad_cap * slope_tan).astype(jnp.bfloat16)
    head_out = jnp.einsum(
        "krd,krv->dv", gathered, jnp.stack([dlogit_tan, dlogit]), preferred_element_type=jnp.float32
    )

    first_row = lax.axis_index("tok") * rows_here
    own_total = lax.dynamic_slice_in_dim(row_total, first_row, rows_here)
    own_mean = lax.dynamic_slice_in_dim(mean_tangent, first_row, rows_here)
    own_factor = lax.dynamic_slice_in_dim(factor, first_row, rows_here)
    scale_main = (own_factor / own_total)[:, None]
    scale_mean = ((2.0 * zloss_weight - own_factor) * own_mean / own_total)[:, None]
    hidden_out = scale_main * reduced[0] + scale_mean * reduced[1] - reduced[2]
    return (head_out, hidden_out)


def solution(mesh):
    tok_size, voc_size = mesh.devices.shape
    x_size = 4 if voc_size % 4 == 0 else 1
    split = Mesh(np.asarray(mesh.devices).reshape(tok_size, voc_size // x_size, x_size), ("tok", "vy", "vx"))
    voc = ("vy", "vx")
    return jax.shard_map(
        local,
        mesh=split,
        in_specs=(
            P("tok", voc),
            P(None, ("tok",) + voc),
            P(),
            P("tok", voc),
            P(None, ("tok",) + voc),
        ),
        out_specs=(P(None, ("tok",) + voc), P("tok", voc)),
        check_vma=False,
    )
```

```python
import jax
import jax.numpy as jnp
from jax import lax
import numpy as np
from jax.sharding import Mesh, PartitionSpec as P

softcap_value = 30.0
zloss_weight = 0.0001


def local(hidden, head, targets, probe_hidden, probe_head):
    voc_count = lax.axis_size("vy") * lax.axis_size("vx")
    vocab_width = head.shape[1]
    rows_here = hidden.shape[0]
    stacked = jnp.stack([hidden, probe_hidden])
    copies = jnp.broadcast_to(stacked[None], (voc_count,) + stacked.shape)
    blocks = lax.all_to_all(copies, ("vy", "vx"), 0, 0, tiled=True)
    features = blocks.transpose(1, 2, 0, 3).reshape(2, rows_here, voc_count * stacked.shape[2])
    gathered = lax.all_gather(features, "tok", axis=1, tiled=True)
    row_hidden = gathered[0]
    row_probe = gathered[1]
    logits = jnp.dot(row_hidden, head, preferred_element_type=jnp.float32)
    tangent = jnp.dot(row_probe, head, preferred_element_type=jnp.float32) + jnp.dot(
        row_hidden, probe_head, preferred_element_type=jnp.float32
    )
    capped = jnp.tanh(logits / softcap_value)
    cap_slope = 1.0 - capped * capped
    exponent = jnp.exp(softcap_value * capped)
    cap_tangent = cap_slope * tangent
    slope_tan = -2.0 / softcap_value * capped * cap_slope * tangent
    voc_index = lax.axis_index("vy") * lax.axis_size("vx") + lax.axis_index("vx")
    offset = (lax.axis_index("tok") * voc_count + voc_index) * vocab_width
    columns = offset + lax.iota(jnp.int32, vocab_width)
    onehot = (targets[:, None] == columns[None, :]).astype(jnp.float32)

    weighted_slope = exponent * cap_slope
    weighted_tan = exponent * (cap_slope * cap_tangent + slope_tan)
    hi = lax.Precision.HIGHEST
    by_probe = lax.dot_general(
        jnp.stack([weighted_slope, onehot * cap_slope]), probe_head.astype(jnp.float32),
        (((2,), (1,)), ((), ())), precision=hi, preferred_element_type=jnp.float32,
    )
    by_head = lax.dot_general(
        jnp.stack([weighted_tan, weighted_slope, onehot * slope_tan]), head.astype(jnp.float32),
        (((2,), (1,)), ((), ())), precision=hi, preferred_element_type=jnp.float32,
    )
    partials = jnp.stack([by_probe[0] + by_head[0], by_head[1], by_probe[1] + by_head[2]])

    local_stats = jnp.stack([jnp.sum(exponent, axis=1), jnp.sum(exponent * cap_tangent, axis=1)])
    partials, local_stats = lax.optimization_barrier((partials, local_stats))
    summed = lax.psum_scatter(partials, "tok", scatter_dimension=1, tiled=True)
    stats = lax.psum(lax.psum(lax.psum(local_stats, "tok"), "vy"), "vx")
    kinds, rows, width = summed.shape
    blocks = summed.reshape(kinds, rows, voc_count, width // voc_count).transpose(2, 0, 1, 3)
    reduced = jnp.sum(lax.all_to_all(blocks, ("vy", "vx"), 0, 0, tiled=True), axis=0)
    row_total = stats[0]
    probability = exponent / row_total[:, None]
    mean_tangent = stats[1] / row_total
    factor = 1.0 + 2.0 * zloss_weight * jnp.log(row_total)
    grad_cap = factor[:, None] * probability - onehot
    grad_tan = probability * (
        factor[:, None] * (cap_tangent - mean_tangent[:, None])
        + 2.0 * zloss_weight * mean_tangent[:, None]
    )
    dlogit = (grad_cap * cap_slope).astype(jnp.bfloat16)
    dlogit_tan = (grad_tan * cap_slope + grad_cap * slope_tan).astype(jnp.bfloat16)
    head_out = jnp.einsum(
        "krd,krv->dv", gathered, jnp.stack([dlogit_tan, dlogit]), preferred_element_type=jnp.float32
    )

    first_row = lax.axis_index("tok") * rows_here
    own_total = lax.dynamic_slice_in_dim(row_total, first_row, rows_here)
    own_mean = lax.dynamic_slice_in_dim(mean_tangent, first_row, rows_here)
    own_factor = lax.dynamic_slice_in_dim(factor, first_row, rows_here)
    scale_main = (own_factor / own_total)[:, None]
    scale_mean = ((2.0 * zloss_weight - own_factor) * own_mean / own_total)[:, None]
    hidden_out = scale_main * reduced[0] + scale_mean * reduced[1] - reduced[2]
    return (head_out, hidden_out)


def solution(mesh):
    tok_size, voc_size = mesh.devices.shape
    x_size = 4 if voc_size % 4 == 0 else 1
    split = Mesh(np.asarray(mesh.devices).reshape(tok_size, voc_size // x_size, x_size), ("tok", "vy", "vx"))
    voc = ("vy", "vx")
    return jax.shard_map(
        local,
        mesh=split,
        in_specs=(
            P("tok", voc),
            P(None, ("tok",) + voc),
            P(),
            P("tok", voc),
            P(None, ("tok",) + voc),
        ),
        out_specs=(P(None, ("tok",) + voc), P("tok", voc)),
        check_vma=False,
    )
```

```python
import jax
import jax.numpy as jnp
from jax import lax
import numpy as np
from jax.sharding import Mesh, PartitionSpec as P

softcap_value = 30.0
zloss_weight = 0.0001


def local(hidden, head, targets, probe_hidden, probe_head):
    voc_count = lax.axis_size("vy") * lax.axis_size("vx")
    vocab_width = head.shape[1]
    rows_here = hidden.shape[0]
    stacked = jnp.stack([hidden, probe_hidden])
    copies = jnp.broadcast_to(stacked[None], (voc_count,) + stacked.shape)
    blocks = lax.all_to_all(copies, ("vy", "vx"), 0, 0, tiled=True)
    features = blocks.transpose(1, 2, 0, 3).reshape(2, rows_here, voc_count * stacked.shape[2])
    gathered = lax.all_gather(features, ("tz", "tc"), axis=1, tiled=True)
    row_hidden = gathered[0]
    row_probe = gathered[1]
    logits = jnp.dot(row_hidden, head, preferred_element_type=jnp.float32)
    tangent = jnp.dot(row_probe, head, preferred_element_type=jnp.float32) + jnp.dot(
        row_hidden, probe_head, preferred_element_type=jnp.float32
    )
    capped = jnp.tanh(logits / softcap_value)
    cap_slope = 1.0 - capped * capped
    exponent = jnp.exp(softcap_value * capped)
    cap_tangent = cap_slope * tangent
    slope_tan = -2.0 / softcap_value * capped * cap_slope * tangent
    voc_index = lax.axis_index("vy") * lax.axis_size("vx") + lax.axis_index("vx")
    offset = ((lax.axis_index("tz") * lax.axis_size("tc") + lax.axis_index("tc")) * voc_count + voc_index) * vocab_width
    columns = offset + lax.iota(jnp.int32, vocab_width)
    onehot = (targets[:, None] == columns[None, :]).astype(jnp.float32)

    weighted_slope = exponent * cap_slope
    weighted_tan = exponent * (cap_slope * cap_tangent + slope_tan)
    hi = lax.Precision.HIGHEST
    by_probe = lax.dot_general(
        jnp.stack([weighted_slope, onehot * cap_slope]), probe_head.astype(jnp.float32),
        (((2,), (1,)), ((), ())), precision=hi, preferred_element_type=jnp.float32,
    )
    by_head = lax.dot_general(
        jnp.stack([weighted_tan, weighted_slope, onehot * slope_tan]), head.astype(jnp.float32),
        (((2,), (1,)), ((), ())), precision=hi, preferred_element_type=jnp.float32,
    )
    partials = jnp.stack([by_probe[0] + by_head[0], by_head[1], by_probe[1] + by_head[2]])

    local_stats = jnp.stack([jnp.sum(exponent, axis=1), jnp.sum(exponent * cap_tangent, axis=1)])
    partials, local_stats = lax.optimization_barrier((partials, local_stats))
    summed = lax.psum_scatter(partials, ("tz", "tc"), scatter_dimension=1, tiled=True)
    stats = lax.psum(lax.psum(lax.psum(lax.psum(local_stats, "tc"), "tz"), "vy"), "vx")
    kinds, rows, width = summed.shape
    blocks = summed.reshape(kinds, rows, voc_count, width // voc_count).transpose(2, 0, 1, 3)
    reduced = jnp.sum(lax.all_to_all(blocks, ("vy", "vx"), 0, 0, tiled=True), axis=0)
    row_total = stats[0]
    probability = exponent / row_total[:, None]
    mean_tangent = stats[1] / row_total
    factor = 1.0 + 2.0 * zloss_weight * jnp.log(row_total)
    grad_cap = factor[:, None] * probability - onehot
    grad_tan = probability * (
        factor[:, None] * (cap_tangent - mean_tangent[:, None])
        + 2.0 * zloss_weight * mean_tangent[:, None]
    )
    dlogit = (grad_cap * cap_slope).astype(jnp.bfloat16)
    dlogit_tan = (grad_tan * cap_slope + grad_cap * slope_tan).astype(jnp.bfloat16)
    head_out = jnp.einsum(
        "krd,krv->dv", gathered, jnp.stack([dlogit_tan, dlogit]), preferred_element_type=jnp.float32
    )

    first_row = (lax.axis_index("tz") * lax.axis_size("tc") + lax.axis_index("tc")) * rows_here
    own_total = lax.dynamic_slice_in_dim(row_total, first_row, rows_here)
    own_mean = lax.dynamic_slice_in_dim(mean_tangent, first_row, rows_here)
    own_factor = lax.dynamic_slice_in_dim(factor, first_row, rows_here)
    scale_main = (own_factor / own_total)[:, None]
    scale_mean = ((2.0 * zloss_weight - own_factor) * own_mean / own_total)[:, None]
    hidden_out = scale_main * reduced[0] + scale_mean * reduced[1] - reduced[2]
    return (head_out, hidden_out)


def solution(mesh):
    tok_size, voc_size = mesh.devices.shape
    c_size = 2 if tok_size % 2 == 0 else 1
    x_size = 4 if voc_size % 4 == 0 else 1
    split = Mesh(
        np.asarray(mesh.devices).reshape(tok_size // c_size, c_size, voc_size // x_size, x_size),
        ("tz", "tc", "vy", "vx"),
    )
    tok = ("tz", "tc")
    voc = ("vy", "vx")
    return jax.shard_map(
        local,
        mesh=split,
        in_specs=(
            P(tok, voc),
            P(None, tok + voc),
            P(),
            P(tok, voc),
            P(None, tok + voc),
        ),
        out_specs=(P(None, tok + voc), P(tok, voc)),
        check_vma=False,
    )
```

```python
import jax
import jax.numpy as jnp
from jax import lax
import numpy as np
from jax.sharding import Mesh, PartitionSpec as P

softcap_value = 30.0
zloss_weight = 0.0001


def local(hidden, head, targets, probe_hidden, probe_head):
    voc_count = lax.axis_size("vy") * lax.axis_size("vx")
    vocab_width = head.shape[1]
    rows_here = hidden.shape[0]
    stacked = jnp.stack([hidden, probe_hidden])
    copies = jnp.broadcast_to(stacked[None], (voc_count,) + stacked.shape)
    blocks = lax.all_to_all(copies, ("vy", "vx"), 0, 0, tiled=True)
    features = blocks.transpose(1, 2, 0, 3).reshape(2, rows_here, voc_count * stacked.shape[2])
    gathered = lax.all_gather(features, "tok", axis=1, tiled=True)
    row_hidden = gathered[0]
    row_probe = gathered[1]
    logits = jnp.dot(row_hidden, head, preferred_element_type=jnp.float32)
    tangent = jnp.dot(row_probe, head, preferred_element_type=jnp.float32) + jnp.dot(
        row_hidden, probe_head, preferred_element_type=jnp.float32
    )
    capped = jnp.tanh(logits / softcap_value)
    cap_slope = 1.0 - capped * capped
    exponent = jnp.exp(softcap_value * capped)
    cap_tangent = cap_slope * tangent
    slope_tan = -2.0 / softcap_value * capped * cap_slope * tangent
    voc_index = lax.axis_index("vy") * lax.axis_size("vx") + lax.axis_index("vx")
    offset = (lax.axis_index("tok") * voc_count + voc_index) * vocab_width
    columns = offset + lax.iota(jnp.int32, vocab_width)
    onehot = (targets[:, None] == columns[None, :]).astype(jnp.float32)

    weighted_slope = exponent * cap_slope
    weighted_tan = exponent * (cap_slope * cap_tangent + slope_tan)
    hi = lax.Precision.HIGH
    by_probe = lax.dot_general(
        jnp.stack([weighted_slope, onehot * cap_slope]), probe_head.astype(jnp.float32),
        (((2,), (1,)), ((), ())), precision=hi, preferred_element_type=jnp.float32,
    )
    by_head = lax.dot_general(
        jnp.stack([weighted_tan, weighted_slope, onehot * slope_tan]), head.astype(jnp.float32),
        (((2,), (1,)), ((), ())), precision=hi, preferred_element_type=jnp.float32,
    )
    partials = jnp.stack([by_probe[0] + by_head[0], by_head[1], by_probe[1] + by_head[2]])

    local_stats = jnp.stack([jnp.sum(exponent, axis=1), jnp.sum(exponent * cap_tangent, axis=1)])
    partials, local_stats = lax.optimization_barrier((partials, local_stats))
    summed = lax.psum_scatter(partials, "tok", scatter_dimension=1, tiled=True)
    stats = lax.psum(lax.psum(lax.psum(local_stats, "tok"), "vy"), "vx")
    kinds, rows, width = summed.shape
    blocks = summed.reshape(kinds, rows, voc_count, width // voc_count).transpose(2, 0, 1, 3)
    reduced = jnp.sum(lax.all_to_all(blocks, ("vy", "vx"), 0, 0, tiled=True), axis=0)
    row_total = stats[0]
    probability = exponent / row_total[:, None]
    mean_tangent = stats[1] / row_total
    factor = 1.0 + 2.0 * zloss_weight * jnp.log(row_total)
    grad_cap = factor[:, None] * probability - onehot
    grad_tan = probability * (
        factor[:, None] * (cap_tangent - mean_tangent[:, None])
        + 2.0 * zloss_weight * mean_tangent[:, None]
    )
    dlogit = (grad_cap * cap_slope).astype(jnp.bfloat16)
    dlogit_tan = (grad_tan * cap_slope + grad_cap * slope_tan).astype(jnp.bfloat16)
    head_out = jnp.einsum(
        "krd,krv->dv", gathered, jnp.stack([dlogit_tan, dlogit]), preferred_element_type=jnp.float32
    )

    first_row = lax.axis_index("tok") * rows_here
    own_total = lax.dynamic_slice_in_dim(row_total, first_row, rows_here)
    own_mean = lax.dynamic_slice_in_dim(mean_tangent, first_row, rows_here)
    own_factor = lax.dynamic_slice_in_dim(factor, first_row, rows_here)
    scale_main = (own_factor / own_total)[:, None]
    scale_mean = ((2.0 * zloss_weight - own_factor) * own_mean / own_total)[:, None]
    hidden_out = scale_main * reduced[0] + scale_mean * reduced[1] - reduced[2]
    return (head_out, hidden_out)


def solution(mesh):
    tok_size, voc_size = mesh.devices.shape
    x_size = 4 if voc_size % 4 == 0 else 1
    split = Mesh(np.asarray(mesh.devices).reshape(tok_size, voc_size // x_size, x_size), ("tok", "vy", "vx"))
    voc = ("vy", "vx")
    return jax.shard_map(
        local,
        mesh=split,
        in_specs=(
            P("tok", voc),
            P(None, ("tok",) + voc),
            P(),
            P("tok", voc),
            P(None, ("tok",) + voc),
        ),
        out_specs=(P(None, ("tok",) + voc), P("tok", voc)),
        check_vma=False,
    )
```
